32 devices in a mesh: chan: 4 (over z), sub: 8 (over y, x, core).
Axes of the slice: x: 2, y: 2, z: 4, core: 2. Of those that a mesh axis runs over, the one named last changes fastest.
Arguments:
- visibilities: float32 [2, 64, 1024], P(None, 'sub', 'chan'), may hold values from -6 to 6
- uv_offset: float32 [2, 64, 1024], P(None, 'sub', 'chan'), may hold values from -9 to 9
- chan_index: int32 [64, 1024], P('sub', 'chan'), may hold values from 0 to 4095
- counts: int32 [64, 4], P('sub', 'chan'), may hold values from 1 to 256, as said below
- row_tile: int32 [64], P('sub'), may hold values from 0 to 7
- col_tile: int32 [64], P('sub'), may hold values from 0 to 63
- primary_beam: float32 [2048, 2048], P(('chan', 'sub')), may hold values from 0.2 to 1
- model_image: float32 [2048, 2048], P(('chan', 'sub')), may hold values from -3 to 3
Outputs:
- new_model: float32 [2048, 2048], P(('chan', 'sub'))
- predicted: float32 [2, 64, 1024], P(None, 'sub', 'chan')
The draws below stay inside these ranges and needn't reach their ends.
Inputs may be any that keep to these rules, and one draw needn't show every extreme that they name: `counts`: the number of leading slots, of the 256 slots of a subgrid in a channel shard, that hold visibilities; later slots are padding and are ignored; some subgrid in some shard has all 256 slots filled.
All inputs are finite; a program needn't handle non-finite values.
Results may differ from the reference program's by a relative error of at most 0.0003.
Values sent between devices are 32-bit elements; how exact they have to be, the bound alone decides.
No kernel may reach another device: no remote copies, remote signals or barrier semaphores. Data moves between devices by JAX's collectives and lax.ppermute only.
A program may use at most 64 MiB of HBM per device.

```python
import math
import jax
import jax.numpy as jnp
from jax import lax

NF = 2048
SG = 32
CH_DEV = 4096
SUB_DEV = 8
CAP = 256
SHARDS = 4
SUBGRIDS = 64
VIS_SLOTS = 1024
ROW_DEV = 256
ROW_TILES = 8
COL_TILES = 64


def draw_counts(key, part):
    owners = SUBGRIDS // SUB_DEV
    shards = VIS_SLOTS // CAP
    key_cap, key_fill, key_owner, key_sub, key_shard = jax.random.split(key, 5)
    device_cap = jax.random.randint(key_cap, (owners, 1, shards), CAP // 4, CAP + 1)
    lowest = jnp.maximum(device_cap // 2, 1)
    spread = jax.random.randint(key_fill, (owners, SUB_DEV, shards), 0, 1 << 20)
    filled = lowest + spread % (device_cap - lowest + 1)
    peak_owner = jax.random.randint(key_owner, (), 0, owners)
    peak_sub = jax.random.randint(key_sub, (), 0, SUB_DEV)
    peak_shard = jax.random.randint(key_shard, (), 0, shards)
    filled = filled.at[peak_owner, peak_sub, peak_shard].set(CAP)
    return filled.reshape(owners * SUB_DEV, shards).astype(jnp.int32)


def touch_ends(result, rng, least, high):
    place = [jax.random.randint(jax.random.fold_in(rng, axis), (), 0, length) for axis, length in enumerate(result.shape)]
    longest = result.shape.index(max(result.shape))
    neighbour = place[:longest] + [(place[longest] + 1) % result.shape[longest]] + place[longest + 1:]
    return result.at[tuple(place)].set(least).at[tuple(neighbour)].set(high)


def block_levels(key, dims, pieces, smallest, largest):
    def one(dim, blocks):
        steps = jax.random.uniform(jax.random.fold_in(jax.random.fold_in(key, 6), dim), (blocks,), jnp.float32, smallest / len(pieces), largest / len(pieces))
        return jnp.repeat(jnp.exp(steps), dims[dim] // blocks).reshape((-1,) + (1,) * (len(dims) - dim - 1))

    level = one(*pieces[0])
    for cut in pieces[1:]:
        level = level * one(*cut)
    return level


def bell_draw(stream_key, shape, scale, most, cuts=(), kind=jnp.bfloat16):
    values = jax.random.normal(stream_key, shape, jnp.float32) * scale
    if len(cuts) > 0:
        values = block_levels(stream_key, shape, cuts, -0.22, 0.18) * values
    return jnp.clip(values, min=-most, max=most).astype(kind)


def setup_inputs(seed: int = 0) -> dict:
    arg_keys = jax.random.split(jax.random.key(seed), 9)
    return {
        "visibilities": bell_draw(arg_keys[0], (2, SUBGRIDS, VIS_SLOTS), 1, 6.0, ((1, 8), (2, 4)), jnp.float32),
        "uv_offset": jnp.clip(jax.random.uniform(arg_keys[1], (2, SUBGRIDS, VIS_SLOTS), jnp.float32, -9.0, 9.0) * block_levels(arg_keys[1], (2, SUBGRIDS, VIS_SLOTS), ((1, 8), (2, 4)), -0.4, 0.0), -9.0, 9.0),
        "chan_index": touch_ends(jax.random.randint(arg_keys[2], (SUBGRIDS, VIS_SLOTS), 0, CH_DEV), jax.random.fold_in(arg_keys[2], 1), 0, CH_DEV - 1).astype(jnp.int32),
        "counts": draw_counts(jax.random.fold_in(arg_keys[8], 71), 0),
        "row_tile": touch_ends(jax.random.randint(arg_keys[4], (SUBGRIDS,), 0, ROW_TILES), jax.random.fold_in(arg_keys[4], 1), 0, ROW_TILES - 1).astype(jnp.int32),
        "col_tile": touch_ends(jax.random.randint(arg_keys[5], (SUBGRIDS,), 0, COL_TILES), jax.random.fold_in(arg_keys[5], 1), 0, COL_TILES - 1).astype(jnp.int32),
        "primary_beam": jnp.clip(jnp.exp(math.log(1.0) - 1.609438 * jax.random.uniform(arg_keys[6], (NF, NF), jnp.float32) ** block_levels(arg_keys[6], (NF, NF), ((0, 32),), -0.2, 0.2)), 0.2, 1.0),
        "model_image": bell_draw(arg_keys[7], (NF, NF), 0.5, 3.0, ((0, 32),), jnp.float32),
    }


precise = lax.Precision.HIGHEST

def centred_table(polarity):
    counter = jnp.arange(SG, dtype=jnp.int32) - SG // 2
    product = counter[:, None] * counter[None, :] % SG
    phase_angle = polarity * 2.0 * math.pi / SG * product.astype(jnp.float32)
    return (jnp.cos(phase_angle), jnp.sin(phase_angle))

def pixel_terms():
    counter = jnp.arange(SG, dtype=jnp.float32)
    pixel_coords = (counter - SG // 2) / SG
    taper_row = 1.0 - 0.8 * ((2.0 * counter + 1.0 - SG) / SG) ** 2
    return (pixel_coords, taper_row[:, None] * taper_row[None, :])

def mat_product(left, right):
    return jnp.dot(left, right, precision=precise, preferred_element_type=jnp.float32)

def complex_product(left_re, left_im, right_re, right_im):
    real_part = mat_product(left_re, right_re) - mat_product(left_im, right_im)
    imag_part = mat_product(left_re, right_im) + mat_product(left_im, right_re)
    return (real_part, imag_part)

def phasors(u_row, v_row, pixel_coords):
    a_angle = 2.0 * math.pi * u_row[:, None] * pixel_coords[None, :]
    b_angle = 2.0 * math.pi * v_row[:, None] * pixel_coords[None, :]
    return (jnp.cos(a_angle), jnp.sin(a_angle), jnp.cos(b_angle), jnp.sin(b_angle))

def reference(visibilities, uv_offset, chan_index, counts, row_tile, col_tile, primary_beam, model_image):
    pixel_coords, taper_grid = pixel_terms()
    slot_index = jnp.arange(VIS_SLOTS, dtype=jnp.int32)
    shard_of = slot_index // CAP
    live_mask = ((slot_index % CAP)[None, :] < jnp.repeat(counts, CAP, axis=1)).astype(jnp.float32)
    global_chan = shard_of[None, :] * CH_DEV + chan_index
    freq_scale = 1.0 + 0.5 * global_chan.astype(jnp.float32) / (SHARDS * CH_DEV)
    u_cells = uv_offset[0] * freq_scale
    v_cells = uv_offset[1] * freq_scale
    down_cos, down_sin = centred_table(-1)
    up_cos, up_sin = centred_table(1)

    def grid_one(bundle):
        vis_re, vis_im, u_row, v_row, live_row = bundle
        a_cos, a_sin, b_cos, b_sin = phasors(u_row, v_row, pixel_coords)
        weight_re = (vis_re * live_row)[:, None]
        weight_im = (vis_im * live_row)[:, None]
        wb_re = weight_re * b_cos - weight_im * b_sin
        wb_im = weight_re * b_sin + weight_im * b_cos
        image_re, image_im = complex_product(wb_re.T, wb_im.T, a_cos, a_sin)
        image_re = image_re * taper_grid
        image_im = image_im * taper_grid
        left_re, left_im = complex_product(down_cos, down_sin, image_re, image_im)
        return complex_product(left_re, left_im, down_cos, down_sin)
    win_re, win_im = lax.map(grid_one, (visibilities[0], visibilities[1], u_cells, v_cells, live_mask))
    owner_index = jnp.arange(SUBGRIDS, dtype=jnp.int32) // SUB_DEV
    row_base = owner_index * ROW_DEV + SG * row_tile
    offsets = jnp.arange(SG, dtype=jnp.int32)
    row_index = row_base[:, None, None] + offsets[None, :, None]
    col_index = (SG * col_tile)[:, None, None] + offsets[None, None, :]
    grid_re = jnp.zeros((NF, NF), jnp.float32).at[row_index, col_index].add(win_re)
    grid_im = jnp.zeros((NF, NF), jnp.float32).at[row_index, col_index].add(win_im)
    spectrum = jnp.fft.ifft2(lax.complex(grid_re, grid_im))
    dirty_image = jnp.real(spectrum).T * (NF * NF) / (SG * SG * math.sqrt(SUBGRIDS * CAP * SHARDS))
    shifted = model_image + primary_beam * dirty_image
    new_model = jnp.sign(shifted) * jnp.maximum(jnp.abs(shifted) - 0.25, 0.0)
    model_grid = jnp.fft.fft2(new_model.T) / NF
    back_re = jnp.real(model_grid)[row_index, col_index]
    back_im = jnp.imag(model_grid)[row_index, col_index]

    def predict_one(bundle):
        window_re, window_im, u_row, v_row, live_row = bundle
        left_re, left_im = complex_product(up_cos.T, up_sin.T, window_re, window_im)
        image_re, image_im = complex_product(left_re, left_im, up_cos, up_sin)
        image_re = image_re * taper_grid / SG
        image_im = image_im * taper_grid / SG
        a_cos, a_sin, b_cos, b_sin = phasors(u_row, v_row, pixel_coords)
        inner_re, inner_im = complex_product(a_cos, -a_sin, image_re.T, image_im.T)
        pred_re = lax.optimization_barrier(jnp.sum(b_cos * inner_re + b_sin * inner_im, axis=1))
        pred_im = lax.optimization_barrier(jnp.sum(b_cos * inner_im - b_sin * inner_re, axis=1))
        factor = 4.0 / SG * live_row
        return (pred_re * factor, pred_im * factor)
    pred_re, pred_im = lax.map(predict_one, (back_re, back_im, u_cells, v_cells, live_mask))
    return (new_model, jnp.stack([pred_re, pred_im]))
```

```python
import functools
import math

import jax
import jax.numpy as jnp
import numpy as np
from jax import lax
from jax.experimental import pallas as pl
from jax.experimental.pallas import tpu as pltpu
from jax.sharding import PartitionSpec as P

SG = 32
CH_DEV = 4096
SUB_DEV = 8
CAP = 256
LANES = 128
RADIX = 16


precise = lax.Precision.HIGHEST


def complex_einsum(formula, left_re, left_im, right_re, right_im):
    if right_im is None:
        real_part = jnp.einsum(formula, left_re, right_re, precision=precise)
        imag_part = jnp.einsum(formula, left_im, right_re, precision=precise)
        return (real_part, imag_part)
    real_part = jnp.einsum(formula, left_re, right_re, precision=precise) - jnp.einsum(
        formula, left_im, right_im, precision=precise
    )
    imag_part = jnp.einsum(formula, left_re, right_im, precision=precise) + jnp.einsum(
        formula, left_im, right_re, precision=precise
    )
    return (real_part, imag_part)


def root_table(leading, trailing, modulus, polarity):
    first_index = jnp.arange(leading, dtype=jnp.int32)
    second_index = jnp.arange(trailing, dtype=jnp.int32)
    product = first_index[:, None] * second_index[None, :] % modulus
    phase_angle = polarity * 2.0 * math.pi / modulus * product.astype(jnp.float32)
    return (jnp.cos(phase_angle), jnp.sin(phase_angle))


def split_factor(extent):
    factor = math.isqrt(extent)
    while extent % factor:
        factor -= 1
    return factor


def transform_last(values_re, values_im, polarity):
    extent = values_re.shape[-1]
    inner_count = split_factor(extent)
    outer_count = extent // inner_count
    row_count = values_re.shape[0]
    shaped_re = values_re.reshape(row_count, outer_count, inner_count)
    shaped_im = (
        None if values_im is None else values_im.reshape(row_count, outer_count, inner_count)
    )
    outer_cos, outer_sin = root_table(outer_count, outer_count, outer_count, polarity)
    section_re, section_im = complex_einsum(
        "kn,rnm->rkm", outer_cos, outer_sin, shaped_re, shaped_im
    )
    twist_cos, twist_sin = root_table(outer_count, inner_count, extent, polarity)
    twisted_re = section_re * twist_cos - section_im * twist_sin
    twisted_im = section_re * twist_sin + section_im * twist_cos
    inner_cos, inner_sin = root_table(inner_count, inner_count, inner_count, polarity)
    result_re, result_im = complex_einsum(
        "jm,rkm->rjk", inner_cos, inner_sin, twisted_re, twisted_im
    )
    return (result_re.reshape(row_count, extent), result_im.reshape(row_count, extent))


def centred_table(polarity):
    counter = jnp.arange(SG, dtype=jnp.int32) - SG // 2
    product = counter[:, None] * counter[None, :] % SG
    phase_angle = polarity * 2.0 * math.pi / SG * product.astype(jnp.float32)
    return (jnp.cos(phase_angle), jnp.sin(phase_angle))


def pixel_terms():
    counter = jnp.arange(SG, dtype=jnp.float32)
    pixel_coords = (counter - SG // 2) / SG
    taper_row = 1.0 - 0.8 * ((2.0 * counter + 1.0 - SG) / SG) ** 2
    return (pixel_coords, taper_row[:, None] * taper_row[None, :])


def general_device(
    visibilities, uv_offset, chan_index, counts, row_tile, col_tile, primary_beam, model_image
):
    shards = lax.axis_size("chan")
    owners = lax.axis_size("sub")
    shard_index = lax.axis_index("chan")
    facet_len = primary_beam.shape[1]
    row_dev = facet_len // owners
    band_len = facet_len // shards
    row_tiles = row_dev // SG
    col_tiles = facet_len // SG
    pixel_coords, taper_grid = pixel_terms()
    down_cos, down_sin = centred_table(-1)
    up_cos, up_sin = centred_table(1)
    global_chan = shard_index * CH_DEV + chan_index
    freq_scale = 1.0 + 0.5 * global_chan.astype(jnp.float32) / (shards * CH_DEV)
    u_cells = uv_offset[0] * freq_scale
    v_cells = uv_offset[1] * freq_scale
    row_hot = (row_tile[:, None] == jnp.arange(row_tiles, dtype=jnp.int32)[None, :]).astype(
        jnp.float32
    )
    col_hot = (col_tile[:, None] == jnp.arange(col_tiles, dtype=jnp.int32)[None, :]).astype(
        jnp.float32
    )
    pair_hot = (row_hot[:, :, None] * col_hot[:, None, :]).reshape(SUB_DEV, row_tiles * col_tiles)
    slot_index = jnp.arange(CAP, dtype=jnp.int32)
    live_mask = (slot_index[None, :] < counts).astype(jnp.float32)
    vis_re = visibilities[0] * live_mask
    vis_im = visibilities[1] * live_mask
    a_angle = 2.0 * math.pi * u_cells[:, :, None] * pixel_coords
    b_angle = 2.0 * math.pi * v_cells[:, :, None] * pixel_coords
    terms = (
        live_mask,
        vis_re,
        vis_im,
        jnp.cos(a_angle),
        jnp.sin(a_angle),
        jnp.cos(b_angle),
        jnp.sin(b_angle),
    )
    live_mask, vis_re, vis_im, a_cos, a_sin, b_cos, b_sin = terms
    wb_re = vis_re[:, :, None] * b_cos - vis_im[:, :, None] * b_sin
    wb_im = vis_re[:, :, None] * b_sin + vis_im[:, :, None] * b_cos
    image_re, image_im = complex_einsum("jkq,jkp->jqp", wb_re, wb_im, a_cos, a_sin)
    image_re = image_re * taper_grid
    image_im = image_im * taper_grid
    left_re, left_im = complex_einsum("aq,jqp->jap", down_cos, down_sin, image_re, image_im)
    win_re, win_im = complex_einsum("jap,bp->jab", left_re, left_im, down_cos, down_sin)
    stacked = jnp.concatenate(
        [win_re.reshape(SUB_DEV, SG * SG), win_im.reshape(SUB_DEV, SG * SG)], axis=1
    )
    placed = jnp.dot(pair_hot.T, stacked, precision=precise, preferred_element_type=jnp.float32)
    placed = (
        placed.reshape(row_tiles, col_tiles, 2, SG, SG)
        .transpose(2, 0, 3, 1, 4)
        .reshape(2, row_dev, facet_len)
    )
    band_spec_re, band_spec_im = transform_last(placed[0], placed[1], 1)
    tile_re, tile_im = (
        lax.psum_scatter(band_spec_re, "chan", scatter_dimension=1, tiled=True),
        lax.psum_scatter(band_spec_im, "chan", scatter_dimension=1, tiled=True),
    )
    image_rows_re, image_rows_im = (
        lax.all_to_all(tile_re.T, "sub", split_axis=0, concat_axis=1, tiled=True),
        lax.all_to_all(tile_im.T, "sub", split_axis=0, concat_axis=1, tiled=True),
    )
    sky_re, sky_im = transform_last(image_rows_re, image_rows_im, 1)
    dirty_scale = 1.0 / (SG * SG * math.sqrt(SUB_DEV * owners * CAP * shards))
    dirty_image = sky_re * dirty_scale
    shifted = model_image + primary_beam * dirty_image
    new_model = jnp.sign(shifted) * jnp.maximum(jnp.abs(shifted) - 0.25, 0.0)
    forward_re, forward_im = transform_last(new_model, None, -1)
    back_rows_re, back_rows_im = (
        lax.all_to_all(forward_re, "sub", split_axis=1, concat_axis=0, tiled=True),
        lax.all_to_all(forward_im, "sub", split_axis=1, concat_axis=0, tiled=True),
    )
    grid_band_re = back_rows_re.T
    grid_band_im = back_rows_im.T
    chosen_re = jnp.einsum(
        "jr,ral->jal", row_hot, grid_band_re.reshape(row_tiles, SG, band_len), precision=precise
    )
    chosen_im = jnp.einsum(
        "jr,ral->jal", row_hot, grid_band_im.reshape(row_tiles, SG, band_len), precision=precise
    )
    u_index = col_tile[:, None] * SG + jnp.arange(SG, dtype=jnp.int32)[None, :]
    l_index = shard_index * band_len + jnp.arange(band_len, dtype=jnp.int32)
    product = u_index[:, :, None] * l_index[None, None, :] % facet_len
    phase_angle = -1 * 2.0 * math.pi / facet_len * product.astype(jnp.float32)
    down_col_cos = jnp.cos(phase_angle)
    down_col_sin = jnp.sin(phase_angle)
    part_re, part_im = complex_einsum(
        "jal,jbl->jab", chosen_re, chosen_im, down_col_cos, down_col_sin
    )
    summed_re, summed_im = lax.psum((part_re, part_im), "chan")
    back_win_re = summed_re / facet_len
    back_win_im = summed_im / facet_len
    left_re, left_im = complex_einsum("aq,jab->jqb", up_cos, up_sin, back_win_re, back_win_im)
    model_sub_re, model_sub_im = complex_einsum("jqb,bp->jqp", left_re, left_im, up_cos, up_sin)
    model_sub_re = model_sub_re * taper_grid / SG
    model_sub_im = model_sub_im * taper_grid / SG
    live_mask, vis_re, vis_im, a_cos, a_sin, b_cos, b_sin = terms
    inner_re, inner_im = complex_einsum("jkp,jqp->jkq", a_cos, -a_sin, model_sub_re, model_sub_im)
    pred_re = jnp.sum(b_cos * inner_re + b_sin * inner_im, axis=2)
    pred_im = jnp.sum(b_cos * inner_im - b_sin * inner_re, axis=2)
    factor = 4.0 / SG * live_mask
    pred_re, pred_im = (pred_re * factor, pred_im * factor)
    return (new_model, jnp.stack([pred_re, pred_im]))


def _fit():
    nodes = 0.5 * np.cos(np.pi * (np.arange(400) + 0.5) / 400)
    square = nodes * nodes
    powers = np.vander(square, 9, increasing=True)
    cos_fit = np.linalg.lstsq(powers, np.cos(2 * np.pi * nodes), rcond=None)[0]
    ratio = np.where(nodes == 0, 2 * np.pi, np.sin(2 * np.pi * nodes) / nodes)
    sin_fit = np.linalg.lstsq(powers, ratio, rcond=None)[0]
    return [float(x) for x in cos_fit], [float(x) for x in sin_fit]


COS_FIT, SIN_FIT = _fit()


def cis(turns):
    rest = turns - jnp.round(turns)
    square = rest * rest
    cos = jnp.full_like(rest, COS_FIT[-1])
    sin = jnp.full_like(rest, SIN_FIT[-1])
    for c, s in zip(COS_FIT[-2::-1], SIN_FIT[-2::-1], strict=True):
        cos = cos * square + c
        sin = sin * square + s
    return cos, sin * rest


def halves(x):
    high = x.astype(jnp.bfloat16)
    return high, (x - high.astype(jnp.float32)).astype(jnp.bfloat16)


NN = (((1,), (0,)), ((), ()))
NT = (((1,), (1,)), ((), ()))


def dot3(left, right, dims):
    dot = functools.partial(
        lax.dot_general, dimension_numbers=dims, preferred_element_type=jnp.float32
    )
    return dot(left[0], right[0]) + (dot(left[1], right[0]) + dot(left[0], right[1]))


def window_table():
    a = np.concatenate([np.arange(0, SG, 2), np.arange(1, SG, 2)]) - SG // 2
    q = np.arange(SG) - SG // 2
    taper = 1.0 - 0.8 * ((2.0 * np.arange(SG) + 1.0 - SG) / SG) ** 2
    value = np.exp(-2j * np.pi * np.outer(a, q) / SG) * taper[None, :]
    return np.block([[value.real, -value.imag], [value.imag, value.real]]).astype(np.float32)


def column_table(facet_len, rows):
    p = np.arange(SG) - SG // 2
    b = np.arange(SG)
    taper = 1.0 - 0.8 * ((2.0 * np.arange(SG) + 1.0 - SG) / SG) ** 2
    window = np.exp(-2j * np.pi * np.outer(b - SG // 2, p) / SG) * taper[None, :]
    value = np.exp(2j * np.pi * np.outer(np.arange(facet_len), b) / facet_len) @ window
    value = value.reshape(facet_len // rows, rows, SG)
    top = np.concatenate([value.real, -value.imag], axis=2)
    low = np.concatenate([value.imag, value.real], axis=2)
    return np.concatenate([top, low], axis=1).astype(np.float32)


def phasor_rows(row):
    steps = lax.broadcasted_iota(jnp.int32, (8, CAP), 0).astype(jnp.float32) / SG
    cos, sin = cis(row * steps)
    return cos, sin


def grid_kernel(
    row_ref, col_ref, vis_ref, uv_ref, chan_ref, counts_ref, window_ref, out_ref, a_ref, b_ref,
    *, shards, row_tiles
):
    shard = lax.axis_index("chan")
    owner = lax.axis_index("sub")
    chan = (shard * CH_DEV + chan_ref[...]).astype(jnp.float32)
    scale = 1.0 + 0.5 * chan / (shards * CH_DEV)
    slot = lax.broadcasted_iota(jnp.int32, (SUB_DEV, CAP), 1)
    live = (slot < counts_ref[...]).astype(jnp.float32)
    vis_re = vis_ref[0] * live
    vis_im = vis_ref[1] * live
    window = halves(window_ref[...])
    steps = lax.broadcasted_iota(jnp.int32, (8, CAP), 0).astype(jnp.float32) / SG
    far = []
    for axis in range(2):
        cells = uv_ref[axis] * scale
        far.append((cells, cis(cells * 0.25), cis(cells * 0.5)))

    def phasors(axis, j):
        cells, (c8, s8), (c16, s16) = far[axis]
        cos, sin = cis(cells[j : j + 1] * steps)
        c8, s8, c16, s16 = (x[j : j + 1] for x in (c8, s8, c16, s16))
        re = [cos * c16 + sin * s16, cos * c8 + sin * s8, cos, cos * c8 - sin * s8]
        im = [sin * c16 - cos * s16, sin * c8 - cos * s8, sin, sin * c8 + cos * s8]
        return jnp.concatenate(re, axis=0), jnp.concatenate(im, axis=0)

    for j in range(SUB_DEV):
        a_re, a_im = phasors(0, j)
        a_ref[j] = jnp.concatenate([a_re, a_im], axis=0)
        b_re, b_im = phasors(1, j)
        hat = dot3(window, halves(jnp.concatenate([b_re, b_im], axis=0)), NN)
        b_ref[j] = hat
        hat_re, hat_im = hat[:SG], hat[SG:]
        re, im = vis_re[j : j + 1], vis_im[j : j + 1]
        left = jnp.concatenate([re * hat_re - im * hat_im, re * hat_im + im * hat_re], axis=1)
        right = jnp.concatenate(
            [jnp.concatenate([a_re, -a_im], axis=1), jnp.concatenate([a_im, a_re], axis=1)], axis=0
        )
        image = dot3(halves(left), halves(right), NT)
        out_ref[0:RADIX, j, :] = jnp.concatenate([image[:RADIX], image[RADIX:]], axis=1)
    line = lax.broadcasted_iota(jnp.int32, (SUB_DEV, LANES), 0)
    lane = lax.broadcasted_iota(jnp.int32, (SUB_DEV, LANES), 1)
    info = jnp.zeros((SUB_DEV, LANES), jnp.int32)
    for j in range(SUB_DEV):
        info = jnp.where((line == j) & (lane == 0), owner * row_tiles + row_ref[j], info)
        info = jnp.where((line == j) & (lane == 1), col_ref[j], info)
    out_ref[RADIX] = info.astype(jnp.float32)


def real_from_half(h0, h8, hr, hi):
    c1, c3, r = math.cos(math.pi / 8), math.cos(3 * math.pi / 8), math.sqrt(0.5)
    (r1, r2, r3, r4, r5, r6, r7), (i1, i2, i3, i4, i5, i6, i7) = hr, hi
    p, q, s, d = h0 + h8, h0 - h8, r2 + r6, r * (r2 - r6)
    t = p + r4
    even = [t + s, q + d, p - r4, q - d, t - s]
    s17, d17, s35, d35 = r1 + r7, r1 - r7, r3 + r5, r3 - r5
    odd = [s17 + s35, c1 * d17 + c3 * d35, r * (s17 - s35), c3 * d17 - c1 * d35]
    cos = [even[m] + odd[m] for m in range(4)] + [even[4]] + [even[m] - odd[m] for m in (3, 2, 1, 0)]
    s17, d17, s35, d35 = i1 + i7, i1 - i7, i3 + i5, i3 - i5
    odd = [None, c3 * s17 + c1 * s35, r * (d17 + d35), c1 * s17 - c3 * s35, d17 - d35]
    s26 = r * (i2 + i6)
    even = [None, s26 + i4, i2 - i6, s26 - i4]
    sin = [None] + [odd[m] + even[m] for m in (1, 2, 3)] + [odd[4]] + [odd[m] - even[m] for m in (3, 2, 1)]
    out = [cos[0]] + [cos[m] - sin[m] for m in range(1, 8)] + [cos[8]]
    return out + [cos[m] + sin[m] for m in range(7, 0, -1)]


def half_from_real(x):
    c1, c3, r = math.cos(math.pi / 8), math.cos(3 * math.pi / 8), math.sqrt(0.5)
    s = [None] + [x[m] + x[16 - m] for m in range(1, 8)]
    d = [None] + [x[m] - x[16 - m] for m in range(1, 8)]
    p, q = x[0] + x[8], x[0] - x[8]
    s17, d17, s35, d35, s26, d26 = s[1] + s[7], s[1] - s[7], s[3] + s[5], s[3] - s[5], s[2] + s[6], r * (s[2] - s[6])
    t = p + s[4]
    even = [t + s26, q + d26, p - s[4], q - d26, t - s26]
    odd = [s17 + s35, c1 * d17 + c3 * d35, r * (s17 - s35), c3 * d17 - c1 * d35]
    re = [even[m] + odd[m] for m in range(4)] + [even[4]] + [even[m] - odd[m] for m in (3, 2, 1, 0)]
    s17, d17, s35, d35 = d[1] + d[7], d[1] - d[7], d[3] + d[5], d[3] - d[5]
    odd = [None, c3 * s17 + c1 * s35, r * (d17 + d35), c1 * s17 - c3 * s35, d17 - d35]
    s26 = r * (d[2] + d[6])
    even = [None, s26 + d[4], d[2] - d[6], s26 - d[4]]
    im = [None] + [odd[m] + even[m] for m in (1, 2, 3)] + [odd[4]] + [odd[m] - even[m] for m in (3, 2, 1)] + [None]
    return re, im


def image_kernel(
    own_ref, pair_ref, table_ref, beam_ref, model_ref, new_ref, own_out, pair_out,
    wide_ref, spec_ref, back_ref, *, shards, scale
):
    own_blocks = own_ref.shape[0]
    blocks = [own_ref.at[t] for t in range(own_blocks)] + [pair_ref.at[t] for t in range(own_blocks)]
    rows = beam_ref.shape[0]
    info = jnp.concatenate([b[RADIX] for b in blocks], axis=0) * (1.0 / shards)
    info = jnp.concatenate([info, info], axis=0)
    line = lax.broadcasted_iota(jnp.int32, (LANES, LANES), 0)
    lane = lax.broadcasted_iota(jnp.int32, (LANES, LANES), 1)
    upper = (line >= LANES // 2).astype(jnp.float32)
    fine = 2.0 * info[:, 0:1] + upper
    cos, sin = cis(fine * lane.astype(jnp.float32) * (1.0 / LANES))
    mix = jnp.concatenate(
        [jnp.concatenate([cos, sin], axis=1), jnp.concatenate([-sin, cos], axis=1)], axis=0
    )
    mix = halves(mix)
    column = jnp.broadcast_to(info[:, 1:2], (LANES, LANES)).T[:rows]
    phase_cos, phase_sin = cis(column * line[:rows].astype(jnp.float32) * (1.0 / 64))
    table = jnp.concatenate([table_ref[...], table_ref[...]], axis=1)
    table = jnp.concatenate(
        [jnp.where(lane < LANES // 2, table, 0.0), jnp.where(lane < LANES // 2, 0.0, table)], axis=0
    )
    down = halves(table)
    up = halves(table.T)
    for k in range(RADIX // 2):
        stack = [b[k] for b in blocks] + [b[RADIX // 2 + k] for b in blocks]
        wide = dot3(down, halves(jnp.concatenate(stack, axis=0)), NT)
        for b in range(2):
            re = wide[2 * b * rows : (2 * b + 1) * rows]
            im = wide[(2 * b + 1) * rows : (2 * b + 2) * rows]
            both = jnp.concatenate(
                [re * phase_cos - im * phase_sin, re * phase_sin + im * phase_cos], axis=1
            )
            high, low = halves(both)
            at = pl.ds((2 * k + b) * rows, rows)
            wide_ref[0, at] = high
            wide_ref[1, at] = low
    group = 4 * rows
    for g in range(RADIX // 4):
        at = pl.ds(g * group, group)
        spec_ref[at] = dot3((wide_ref[0, at], wide_ref[1, at]), mix, NN)
    twist = [cis(lax.broadcasted_iota(jnp.int32, (8, LANES), 1).astype(jnp.float32) * (a / (RADIX * LANES))) for a in range(1, RADIX)]

    for tile in range(rows // 8):
        at = lambda a: pl.ds(a * rows + tile * 8, 8)
        re = [spec_ref[at(0), :LANES]]
        im = [None]
        for a in range(1, RADIX):
            x, y = spec_ref[at(a), :LANES], spec_ref[at(a), LANES:]
            c, s = twist[a - 1]
            re.append(x * c - y * s)
            im.append(x * s + y * c)
        hr = [re[a] + re[RADIX - a] for a in range(1, 8)]
        hi = [im[a] - im[RADIX - a] for a in range(1, 8)]
        dirty = real_from_half(re[0], re[8], hr, hi)
        new = []
        for m in range(RADIX):
            where = (slice(tile * 8, tile * 8 + 8), slice(m * LANES, (m + 1) * LANES))
            shifted = model_ref[where] + beam_ref[where] * (dirty[m] * scale)
            value = shifted - jnp.clip(shifted, -0.25, 0.25)
            new_ref[where] = value
            new.append(value)
        re, im = half_from_real(new)
        back_ref[at(0), :LANES] = re[0]
        back_ref[at(0), LANES:] = jnp.zeros_like(re[0])
        for a in range(1, RADIX):
            c, s = twist[a - 1]
            if a == 8:
                back_ref[at(a), :LANES] = re[8] * c
                back_ref[at(a), LANES:] = -(re[8] * s)
                continue
            x, y = (re[a], im[a]) if a < 8 else (re[RADIX - a], -im[RADIX - a])
            back_ref[at(a), :LANES] = x * c - y * s
            back_ref[at(a), LANES:] = -(x * s + y * c)
    for g in range(RADIX // 4):
        at = pl.ds(g * group, group)
        spec_ref[at] = dot3(halves(back_ref[at]), mix, NT)
    for k in range(RADIX // 2):
        stack = []
        for b in range(2):
            at = pl.ds((2 * k + b) * rows, rows)
            re, im = spec_ref[at, :LANES], spec_ref[at, LANES:]
            stack.append(re * phase_cos + im * phase_sin)
            stack.append(im * phase_cos - re * phase_sin)
        part = dot3(up, halves(jnp.concatenate(stack, axis=0)), NN).T
        for h in range(2):
            for t in range(own_blocks):
                first = h * LANES // 2 + t * SUB_DEV
                own_out[t, h * RADIX // 2 + k] = part[first : first + SUB_DEV]
                first += own_blocks * SUB_DEV
                pair_out[t, h * RADIX // 2 + k] = part[first : first + SUB_DEV]


def predict_kernel(x0, x1, x2, x3, a_ref, b_ref, counts_ref, out_ref, *, scale):
    total = (x0[...] + x1[...]) + (x2[...] + x3[...])
    slot = lax.broadcasted_iota(jnp.int32, (1, CAP), 1)
    for j in range(SUB_DEV):
        rows = total[:, j, :]
        left = halves(jnp.concatenate([rows[:, : LANES // 2], rows[:, LANES // 2 :]], axis=0))
        a_re, a_im = a_ref[j, :SG], a_ref[j, SG:]
        inner_re = dot3(left, halves(jnp.concatenate([a_re, a_im], axis=0)), NN)
        inner_im = dot3(left, halves(jnp.concatenate([-a_im, a_re], axis=0)), NN)
        b_re, b_im = b_ref[j, :SG], b_ref[j, SG:]
        factor = jnp.where(slot < counts_ref[j : j + 1], scale, 0.0)
        re = jnp.sum(b_re * inner_re + b_im * inner_im, axis=0, keepdims=True)
        im = jnp.sum(b_re * inner_im - b_im * inner_re, axis=0, keepdims=True)
        out_ref[0, j : j + 1] = re * factor
        out_ref[1, j : j + 1] = im * factor


def swap(x, axis, mask):
    size = lax.axis_size(axis)
    return lax.ppermute(x, axis, [(i, i ^ mask) for i in range(size)])


def fast_device(
    visibilities, uv_offset, chan_index, counts, row_tile, col_tile, primary_beam, model_image
):
    shards = lax.axis_size("chan")
    owners = lax.axis_size("sub")
    rows, facet_len = primary_beam.shape
    f32 = jnp.float32
    vmem = pl.BlockSpec(memory_space=pltpu.VMEM)
    smem = pl.BlockSpec(memory_space=pltpu.SMEM)
    shape = jax.ShapeDtypeStruct
    payload, a_rows, b_rows = pl.pallas_call(
        functools.partial(grid_kernel, shards=shards, row_tiles=facet_len // owners // SG),
        out_shape=(
            shape((RADIX + 1, SUB_DEV, LANES), f32),
            shape((SUB_DEV, 2 * SG, CAP), f32),
            shape((SUB_DEV, 2 * SG, CAP), f32),
        ),
        in_specs=[smem, smem] + [vmem] * 5,
        out_specs=[vmem] * 3,
        name="grid",
    )(row_tile, col_tile, visibilities, uv_offset, chan_index, counts, window_table())
    block = lax.axis_index("chan") * owners + lax.axis_index("sub")
    table = lax.dynamic_index_in_dim(jnp.asarray(column_table(facet_len, rows)), block, 0, False)
    payload = payload + sum(swap(payload, "chan", k) for k in range(1, shards))
    own = jnp.stack([payload] + [swap(payload, "sub", k) for k in range(2, owners, 2)])
    pair = swap(own, "sub", 1)
    part = shape((owners // 2, RADIX, SUB_DEV, LANES), f32)
    new_model, own, pair = pl.pallas_call(
        functools.partial(
            image_kernel,
            shards=shards,
            scale=1.0 / (SG * SG * math.sqrt(SUB_DEV * owners * CAP * shards)),
        ),
        out_shape=(shape((rows, facet_len), f32), part, part),
        in_specs=[vmem] * 5,
        out_specs=[vmem] * 3,
        scratch_shapes=[
            pltpu.VMEM((2, RADIX * rows, 2 * LANES), jnp.bfloat16),
            pltpu.VMEM((RADIX * rows, 2 * LANES), f32),
            pltpu.VMEM((RADIX * rows, 2 * LANES), f32),
        ],
        name="image",
    )(own, pair, table, primary_beam, model_image)
    own = own + swap(pair, "sub", 1)
    part = own[0] + sum(swap(own[k // 2], "sub", k) for k in range(2, owners, 2))
    parts = [part] + [swap(part, "chan", k) for k in range(1, shards)]
    predicted = pl.pallas_call(
        functools.partial(predict_kernel, scale=4.0 / SG / SG / facet_len),
        out_shape=shape((2, SUB_DEV, CAP), f32),
        in_specs=[vmem] * 7,
        out_specs=vmem,
        name="predict",
    )(*parts, a_rows, b_rows, counts)
    return new_model, predicted


def on_device(*arrays):
    shards, owners = lax.axis_size("chan"), lax.axis_size("sub")
    rows, facet_len = arrays[6].shape
    fits = (
        shards == 4
        and owners == 8
        and 2 * rows == LANES
        and facet_len == RADIX * LANES
        and 2 * owners * SUB_DEV == LANES
    )
    return (fast_device if fits else general_device)(*arrays)


def solution(mesh):
    in_specs = (
        P(None, "sub", "chan"),
        P(None, "sub", "chan"),
        P("sub", "chan"),
        P("sub", "chan"),
        P("sub"),
        P("sub"),
        P(("chan", "sub"), None),
        P(("chan", "sub"), None),
    )
    out_specs = (P(("chan", "sub"), None), P(None, "sub", "chan"))
    return jax.shard_map(
        on_device, mesh=mesh, in_specs=in_specs, out_specs=out_specs, check_vma=False
    )
```

```python
import functools
import math

import jax
import jax.numpy as jnp
import numpy as np
from jax import lax
from jax.experimental import pallas as pl
from jax.experimental.pallas import tpu as pltpu
from jax.sharding import PartitionSpec as P

SG = 32
CH_DEV = 4096
SUB_DEV = 8
CAP = 256
LANES = 128
RADIX = 16


precise = lax.Precision.HIGHEST


def complex_einsum(formula, left_re, left_im, right_re, right_im):
    if right_im is None:
        real_part = jnp.einsum(formula, left_re, right_re, precision=precise)
        imag_part = jnp.einsum(formula, left_im, right_re, precision=precise)
        return (real_part, imag_part)
    real_part = jnp.einsum(formula, left_re, right_re, precision=precise) - jnp.einsum(
        formula, left_im, right_im, precision=precise
    )
    imag_part = jnp.einsum(formula, left_re, right_im, precision=precise) + jnp.einsum(
        formula, left_im, right_re, precision=precise
    )
    return (real_part, imag_part)


def root_table(leading, trailing, modulus, polarity):
    first_index = jnp.arange(leading, dtype=jnp.int32)
    second_index = jnp.arange(trailing, dtype=jnp.int32)
    product = first_index[:, None] * second_index[None, :] % modulus
    phase_angle = polarity * 2.0 * math.pi / modulus * product.astype(jnp.float32)
    return (jnp.cos(phase_angle), jnp.sin(phase_angle))


def split_factor(extent):
    factor = math.isqrt(extent)
    while extent % factor:
        factor -= 1
    return factor


def transform_last(values_re, values_im, polarity):
    extent = values_re.shape[-1]
    inner_count = split_factor(extent)
    outer_count = extent // inner_count
    row_count = values_re.shape[0]
    shaped_re = values_re.reshape(row_count, outer_count, inner_count)
    shaped_im = (
        None if values_im is None else values_im.reshape(row_count, outer_count, inner_count)
    )
    outer_cos, outer_sin = root_table(outer_count, outer_count, outer_count, polarity)
    section_re, section_im = complex_einsum(
        "kn,rnm->rkm", outer_cos, outer_sin, shaped_re, shaped_im
    )
    twist_cos, twist_sin = root_table(outer_count, inner_count, extent, polarity)
    twisted_re = section_re * twist_cos - section_im * twist_sin
    twisted_im = section_re * twist_sin + section_im * twist_cos
    inner_cos, inner_sin = root_table(inner_count, inner_count, inner_count, polarity)
    result_re, result_im = complex_einsum(
        "jm,rkm->rjk", inner_cos, inner_sin, twisted_re, twisted_im
    )
    return (result_re.reshape(row_count, extent), result_im.reshape(row_count, extent))


def centred_table(polarity):
    counter = jnp.arange(SG, dtype=jnp.int32) - SG // 2
    product = counter[:, None] * counter[None, :] % SG
    phase_angle = polarity * 2.0 * math.pi / SG * product.astype(jnp.float32)
    return (jnp.cos(phase_angle), jnp.sin(phase_angle))


def pixel_terms():
    counter = jnp.arange(SG, dtype=jnp.float32)
    pixel_coords = (counter - SG // 2) / SG
    taper_row = 1.0 - 0.8 * ((2.0 * counter + 1.0 - SG) / SG) ** 2
    return (pixel_coords, taper_row[:, None] * taper_row[None, :])


def general_device(
    visibilities, uv_offset, chan_index, counts, row_tile, col_tile, primary_beam, model_image
):
    shards = lax.axis_size("chan")
    owners = lax.axis_size("sub")
    shard_index = lax.axis_index("chan")
    facet_len = primary_beam.shape[1]
    row_dev = facet_len // owners
    band_len = facet_len // shards
    row_tiles = row_dev // SG
    col_tiles = facet_len // SG
    pixel_coords, taper_grid = pixel_terms()
    down_cos, down_sin = centred_table(-1)
    up_cos, up_sin = centred_table(1)
    global_chan = shard_index * CH_DEV + chan_index
    freq_scale = 1.0 + 0.5 * global_chan.astype(jnp.float32) / (shards * CH_DEV)
    u_cells = uv_offset[0] * freq_scale
    v_cells = uv_offset[1] * freq_scale
    row_hot = (row_tile[:, None] == jnp.arange(row_tiles, dtype=jnp.int32)[None, :]).astype(
        jnp.float32
    )
    col_hot = (col_tile[:, None] == jnp.arange(col_tiles, dtype=jnp.int32)[None, :]).astype(
        jnp.float32
    )
    pair_hot = (row_hot[:, :, None] * col_hot[:, None, :]).reshape(SUB_DEV, row_tiles * col_tiles)
    slot_index = jnp.arange(CAP, dtype=jnp.int32)
    live_mask = (slot_index[None, :] < counts).astype(jnp.float32)
    vis_re = visibilities[0] * live_mask
    vis_im = visibilities[1] * live_mask
    a_angle = 2.0 * math.pi * u_cells[:, :, None] * pixel_coords
    b_angle = 2.0 * math.pi * v_cells[:, :, None] * pixel_coords
    terms = (
        live_mask,
        vis_re,
        vis_im,
        jnp.cos(a_angle),
        jnp.sin(a_angle),
        jnp.cos(b_angle),
        jnp.sin(b_angle),
    )
    live_mask, vis_re, vis_im, a_cos, a_sin, b_cos, b_sin = terms
    wb_re = vis_re[:, :, None] * b_cos - vis_im[:, :, None] * b_sin
    wb_im = vis_re[:, :, None] * b_sin + vis_im[:, :, None] * b_cos
    image_re, image_im = complex_einsum("jkq,jkp->jqp", wb_re, wb_im, a_cos, a_sin)
    image_re = image_re * taper_grid
    image_im = image_im * taper_grid
    left_re, left_im = complex_einsum("aq,jqp->jap", down_cos, down_sin, image_re, image_im)
    win_re, win_im = complex_einsum("jap,bp->jab", left_re, left_im, down_cos, down_sin)
    stacked = jnp.concatenate(
        [win_re.reshape(SUB_DEV, SG * SG), win_im.reshape(SUB_DEV, SG * SG)], axis=1
    )
    placed = jnp.dot(pair_hot.T, stacked, precision=precise, preferred_element_type=jnp.float32)
    placed = (
        placed.reshape(row_tiles, col_tiles, 2, SG, SG)
        .transpose(2, 0, 3, 1, 4)
        .reshape(2, row_dev, facet_len)
    )
    band_spec_re, band_spec_im = transform_last(placed[0], placed[1], 1)
    tile_re, tile_im = (
        lax.psum_scatter(band_spec_re, "chan", scatter_dimension=1, tiled=True),
        lax.psum_scatter(band_spec_im, "chan", scatter_dimension=1, tiled=True),
    )
    image_rows_re, image_rows_im = (
        lax.all_to_all(tile_re.T, "sub", split_axis=0, concat_axis=1, tiled=True),
        lax.all_to_all(tile_im.T, "sub", split_axis=0, concat_axis=1, tiled=True),
    )
    sky_re, sky_im = transform_last(image_rows_re, image_rows_im, 1)
    dirty_scale = 1.0 / (SG * SG * math.sqrt(SUB_DEV * owners * CAP * shards))
    dirty_image = sky_re * dirty_scale
    shifted = model_image + primary_beam * dirty_image
    new_model = jnp.sign(shifted) * jnp.maximum(jnp.abs(shifted) - 0.25, 0.0)
    forward_re, forward_im = transform_last(new_model, None, -1)
    back_rows_re, back_rows_im = (
        lax.all_to_all(forward_re, "sub", split_axis=1, concat_axis=0, tiled=True),
        lax.all_to_all(forward_im, "sub", split_axis=1, concat_axis=0, tiled=True),
    )
    grid_band_re = back_rows_re.T
    grid_band_im = back_rows_im.T
    chosen_re = jnp.einsum(
        "jr,ral->jal", row_hot, grid_band_re.reshape(row_tiles, SG, band_len), precision=precise
    )
    chosen_im = jnp.einsum(
        "jr,ral->jal", row_hot, grid_band_im.reshape(row_tiles, SG, band_len), precision=precise
    )
    u_index = col_tile[:, None] * SG + jnp.arange(SG, dtype=jnp.int32)[None, :]
    l_index = shard_index * band_len + jnp.arange(band_len, dtype=jnp.int32)
    product = u_index[:, :, None] * l_index[None, None, :] % facet_len
    phase_angle = -1 * 2.0 * math.pi / facet_len * product.astype(jnp.float32)
    down_col_cos = jnp.cos(phase_angle)
    down_col_sin = jnp.sin(phase_angle)
    part_re, part_im = complex_einsum(
        "jal,jbl->jab", chosen_re, chosen_im, down_col_cos, down_col_sin
    )
    summed_re, summed_im = lax.psum((part_re, part_im), "chan")
    back_win_re = summed_re / facet_len
    back_win_im = summed_im / facet_len
    left_re, left_im = complex_einsum("aq,jab->jqb", up_cos, up_sin, back_win_re, back_win_im)
    model_sub_re, model_sub_im = complex_einsum("jqb,bp->jqp", left_re, left_im, up_cos, up_sin)
    model_sub_re = model_sub_re * taper_grid / SG
    model_sub_im = model_sub_im * taper_grid / SG
    live_mask, vis_re, vis_im, a_cos, a_sin, b_cos, b_sin = terms
    inner_re, inner_im = complex_einsum("jkp,jqp->jkq", a_cos, -a_sin, model_sub_re, model_sub_im)
    pred_re = jnp.sum(b_cos * inner_re + b_sin * inner_im, axis=2)
    pred_im = jnp.sum(b_cos * inner_im - b_sin * inner_re, axis=2)
    factor = 4.0 / SG * live_mask
    pred_re, pred_im = (pred_re * factor, pred_im * factor)
    return (new_model, jnp.stack([pred_re, pred_im]))


def _fit():
    nodes = 0.5 * np.cos(np.pi * (np.arange(400) + 0.5) / 400)
    square = nodes * nodes
    powers = np.vander(square, 9, increasing=True)
    cos_fit = np.linalg.lstsq(powers, np.cos(2 * np.pi * nodes), rcond=None)[0]
    ratio = np.where(nodes == 0, 2 * np.pi, np.sin(2 * np.pi * nodes) / nodes)
    sin_fit = np.linalg.lstsq(powers, ratio, rcond=None)[0]
    return [float(x) for x in cos_fit], [float(x) for x in sin_fit]


COS_FIT, SIN_FIT = _fit()


def cis(turns):
    rest = turns - jnp.round(turns)
    square = rest * rest
    cos = jnp.full_like(rest, COS_FIT[-1])
    sin = jnp.full_like(rest, SIN_FIT[-1])
    for c, s in zip(COS_FIT[-2::-1], SIN_FIT[-2::-1], strict=True):
        cos = cos * square + c
        sin = sin * square + s
    return cos, sin * rest


def halves(x):
    high = x.astype(jnp.bfloat16)
    return high, (x - high.astype(jnp.float32)).astype(jnp.bfloat16)


NN = (((1,), (0,)), ((), ()))
NT = (((1,), (1,)), ((), ()))


def dot3(left, right, dims):
    dot = functools.partial(
        lax.dot_general, dimension_numbers=dims, preferred_element_type=jnp.float32
    )
    return dot(left[0], right[0]) + (dot(left[1], right[0]) + dot(left[0], right[1]))


def window_table():
    a = np.concatenate([np.arange(0, SG, 2), np.arange(1, SG, 2)]) - SG // 2
    q = np.arange(SG) - SG // 2
    taper = 1.0 - 0.8 * ((2.0 * np.arange(SG) + 1.0 - SG) / SG) ** 2
    value = np.exp(-2j * np.pi * np.outer(a, q) / SG) * taper[None, :]
    return np.block([[value.real, -value.imag], [value.imag, value.real]]).astype(np.float32)


def column_table(facet_len, rows):
    p = np.arange(SG) - SG // 2
    b = np.arange(SG)
    taper = 1.0 - 0.8 * ((2.0 * np.arange(SG) + 1.0 - SG) / SG) ** 2
    window = np.exp(-2j * np.pi * np.outer(b - SG // 2, p) / SG) * taper[None, :]
    value = np.exp(2j * np.pi * np.outer(np.arange(facet_len), b) / facet_len) @ window
    value = value.reshape(facet_len // rows, rows, SG)
    top = np.concatenate([value.real, -value.imag], axis=2)
    low = np.concatenate([value.imag, value.real], axis=2)
    return np.concatenate([top, low], axis=1).astype(np.float32)


def phasor_rows(row):
    steps = lax.broadcasted_iota(jnp.int32, (8, CAP), 0).astype(jnp.float32) / SG
    cos, sin = cis(row * steps)
    return cos, sin


def grid_kernel(
    row_ref, col_ref, counts_ref, vis_ref, uv_ref, chan_ref, window_ref, out_ref, a_ref, b_ref,
    *, shards, row_tiles
):
    shard = lax.axis_index("chan")
    owner = lax.axis_index("sub")
    chan = (shard * CH_DEV + chan_ref[...]).astype(jnp.float32)
    scale = 1.0 + 0.5 * chan / (shards * CH_DEV)
    slot = lax.broadcasted_iota(jnp.int32, (1, CAP), 1)
    window = halves(window_ref[...])
    steps = lax.broadcasted_iota(jnp.int32, (8, CAP), 0).astype(jnp.float32) / SG
    far = []
    for axis in range(2):
        cells = uv_ref[axis] * scale
        far.append((cells, cis(cells * 0.25), cis(cells * 0.5)))

    def phasors(axis, j):
        cells, (c8, s8), (c16, s16) = far[axis]
        cos, sin = cis(cells[j : j + 1] * steps)
        c8, s8, c16, s16 = (x[j : j + 1] for x in (c8, s8, c16, s16))
        re = [cos * c16 + sin * s16, cos * c8 + sin * s8, cos, cos * c8 - sin * s8]
        im = [sin * c16 - cos * s16, sin * c8 - cos * s8, sin, sin * c8 + cos * s8]
        return jnp.concatenate(re, axis=0), jnp.concatenate(im, axis=0)

    for j in range(SUB_DEV):
        a_re, a_im = phasors(0, j)
        a_ref[j] = jnp.concatenate([a_re, a_im], axis=0)
        b_re, b_im = phasors(1, j)
        hat = dot3(window, halves(jnp.concatenate([b_re, b_im], axis=0)), NN)
        b_ref[j] = hat
        hat_re, hat_im = hat[:SG], hat[SG:]
        live = jnp.where(slot < counts_ref[j], 1.0, 0.0)
        re, im = vis_ref[0, j : j + 1] * live, vis_ref[1, j : j + 1] * live
        left = jnp.concatenate([re * hat_re - im * hat_im, re * hat_im + im * hat_re], axis=1)
        right = jnp.concatenate(
            [jnp.concatenate([a_re, -a_im], axis=1), jnp.concatenate([a_im, a_re], axis=1)], axis=0
        )
        image = dot3(halves(left), halves(right), NT)
        out_ref[0:RADIX, j, :] = jnp.concatenate([image[:RADIX], image[RADIX:]], axis=1)
    line = lax.broadcasted_iota(jnp.int32, (SUB_DEV, LANES), 0)
    lane = lax.broadcasted_iota(jnp.int32, (SUB_DEV, LANES), 1)
    info = jnp.zeros((SUB_DEV, LANES), jnp.int32)
    for j in range(SUB_DEV):
        info = jnp.where((line == j) & (lane == 0), owner * row_tiles + row_ref[j], info)
        info = jnp.where((line == j) & (lane == 1), col_ref[j], info)
    out_ref[RADIX] = info.astype(jnp.float32)


def real_from_half(h0, h8, hr, hi):
    c1, c3, r = math.cos(math.pi / 8), math.cos(3 * math.pi / 8), math.sqrt(0.5)
    (r1, r2, r3, r4, r5, r6, r7), (i1, i2, i3, i4, i5, i6, i7) = hr, hi
    p, q, s, d = h0 + h8, h0 - h8, r2 + r6, r * (r2 - r6)
    t = p + r4
    even = [t + s, q + d, p - r4, q - d, t - s]
    s17, d17, s35, d35 = r1 + r7, r1 - r7, r3 + r5, r3 - r5
    odd = [s17 + s35, c1 * d17 + c3 * d35, r * (s17 - s35), c3 * d17 - c1 * d35]
    cos = [even[m] + odd[m] for m in range(4)] + [even[4]] + [even[m] - odd[m] for m in (3, 2, 1, 0)]
    s17, d17, s35, d35 = i1 + i7, i1 - i7, i3 + i5, i3 - i5
    odd = [None, c3 * s17 + c1 * s35, r * (d17 + d35), c1 * s17 - c3 * s35, d17 - d35]
    s26 = r * (i2 + i6)
    even = [None, s26 + i4, i2 - i6, s26 - i4]
    sin = [None] + [odd[m] + even[m] for m in (1, 2, 3)] + [odd[4]] + [odd[m] - even[m] for m in (3, 2, 1)]
    out = [cos[0]] + [cos[m] - sin[m] for m in range(1, 8)] + [cos[8]]
    return out + [cos[m] + sin[m] for m in range(7, 0, -1)]


def half_from_real(x):
    c1, c3, r = math.cos(math.pi / 8), math.cos(3 * math.pi / 8), math.sqrt(0.5)
    s = [None] + [x[m] + x[16 - m] for m in range(1, 8)]
    d = [None] + [x[m] - x[16 - m] for m in range(1, 8)]
    p, q = x[0] + x[8], x[0] - x[8]
    s17, d17, s35, d35, s26, d26 = s[1] + s[7], s[1] - s[7], s[3] + s[5], s[3] - s[5], s[2] + s[6], r * (s[2] - s[6])
    t = p + s[4]
    even = [t + s26, q + d26, p - s[4], q - d26, t - s26]
    odd = [s17 + s35, c1 * d17 + c3 * d35, r * (s17 - s35), c3 * d17 - c1 * d35]
    re = [even[m] + odd[m] for m in range(4)] + [even[4]] + [even[m] - odd[m] for m in (3, 2, 1, 0)]
    s17, d17, s35, d35 = d[1] + d[7], d[1] - d[7], d[3] + d[5], d[3] - d[5]
    odd = [None, c3 * s17 + c1 * s35, r * (d17 + d35), c1 * s17 - c3 * s35, d17 - d35]
    s26 = r * (d[2] + d[6])
    even = [None, s26 + d[4], d[2] - d[6], s26 - d[4]]
    im = [None] + [odd[m] + even[m] for m in (1, 2, 3)] + [odd[4]] + [odd[m] - even[m] for m in (3, 2, 1)] + [None]
    return re, im


def image_kernel(
    own_ref, pair_ref, table_ref, beam_hbm, model_hbm, new_hbm, own_out, pair_out,
    wide_ref, spec_ref, back_ref, beam_ref, model_ref, new_ref, sems, *, shards, scale
):
    loads = [
        pltpu.make_async_copy(beam_hbm, beam_ref, sems.at[0]),
        pltpu.make_async_copy(model_hbm, model_ref, sems.at[1]),
    ]
    for load in loads:
        load.start()
    own_blocks = own_ref.shape[0]
    blocks = [own_ref.at[t] for t in range(own_blocks)] + [pair_ref.at[t] for t in range(own_blocks)]
    rows = beam_ref.shape[0]
    info = jnp.concatenate([b[RADIX] for b in blocks], axis=0) * (1.0 / shards)
    info = jnp.concatenate([info, info], axis=0)
    line = lax.broadcasted_iota(jnp.int32, (LANES, LANES), 0)
    lane = lax.broadcasted_iota(jnp.int32, (LANES, LANES), 1)
    upper = (line >= LANES // 2).astype(jnp.float32)
    fine = 2.0 * info[:, 0:1] + upper
    cos, sin = cis(fine * lane.astype(jnp.float32) * (1.0 / LANES))
    mix = jnp.concatenate(
        [jnp.concatenate([cos, sin], axis=1), jnp.concatenate([-sin, cos], axis=1)], axis=0
    )
    mix = halves(mix)
    column = jnp.broadcast_to(info[:, 1:2], (LANES, LANES)).T[:rows]
    phase_cos, phase_sin = cis(column * line[:rows].astype(jnp.float32) * (1.0 / 64))
    table = jnp.concatenate([table_ref[...], table_ref[...]], axis=1)
    table = jnp.concatenate(
        [jnp.where(lane < LANES // 2, table, 0.0), jnp.where(lane < LANES // 2, 0.0, table)], axis=0
    )
    down = halves(table)
    up = halves(table.T)
    for k in range(RADIX // 2):
        stack = [b[k] for b in blocks] + [b[RADIX // 2 + k] for b in blocks]
        wide = dot3(down, halves(jnp.concatenate(stack, axis=0)), NT)
        for b in range(2):
            re = wide[2 * b * rows : (2 * b + 1) * rows]
            im = wide[(2 * b + 1) * rows : (2 * b + 2) * rows]
            both = jnp.concatenate(
                [re * phase_cos - im * phase_sin, re * phase_sin + im * phase_cos], axis=1
            )
            high, low = halves(both)
            at = pl.ds((2 * k + b) * rows, rows)
            wide_ref[0, at] = high
            wide_ref[1, at] = low
    group = 4 * rows
    for g in range(RADIX // 4):
        at = pl.ds(g * group, group)
        spec_ref[at] = dot3((wide_ref[0, at], wide_ref[1, at]), mix, NN)
    twist = [cis(lax.broadcasted_iota(jnp.int32, (8, LANES), 1).astype(jnp.float32) * (a / (RADIX * LANES))) for a in range(1, RADIX)]

    for load in loads:
        load.wait()
    for tile in range(rows // 8):
        at = lambda a: pl.ds(a * rows + tile * 8, 8)
        re = [spec_ref[at(0), :LANES]]
        im = [None]
        for a in range(1, RADIX):
            x, y = spec_ref[at(a), :LANES], spec_ref[at(a), LANES:]
            c, s = twist[a - 1]
            re.append(x * c - y * s)
            im.append(x * s + y * c)
        hr = [re[a] + re[RADIX - a] for a in range(1, 8)]
        hi = [im[a] - im[RADIX - a] for a in range(1, 8)]
        dirty = real_from_half(re[0], re[8], hr, hi)
        new = []
        for m in range(RADIX):
            where = (slice(tile * 8, tile * 8 + 8), slice(m * LANES, (m + 1) * LANES))
            shifted = model_ref[where] + beam_ref[where] * (dirty[m] * scale)
            value = shifted - jnp.clip(shifted, -0.25, 0.25)
            new_ref[where] = value
            new.append(value)
        re, im = half_from_real(new)
        back_ref[at(0), :LANES] = re[0]
        back_ref[at(0), LANES:] = jnp.zeros_like(re[0])
        for a in range(1, RADIX):
            c, s = twist[a - 1]
            if a == 8:
                back_ref[at(a), :LANES] = re[8] * c
                back_ref[at(a), LANES:] = -(re[8] * s)
                continue
            x, y = (re[a], im[a]) if a < 8 else (re[RADIX - a], -im[RADIX - a])
            back_ref[at(a), :LANES] = x * c - y * s
            back_ref[at(a), LANES:] = -(x * s + y * c)
    store = pltpu.make_async_copy(new_ref, new_hbm, sems.at[2])
    store.start()
    for g in range(RADIX // 4):
        at = pl.ds(g * group, group)
        spec_ref[at] = dot3(halves(back_ref[at]), mix, NT)
    for k in range(RADIX // 2):
        stack = []
        for b in range(2):
            at = pl.ds((2 * k + b) * rows, rows)
            re, im = spec_ref[at, :LANES], spec_ref[at, LANES:]
            stack.append(re * phase_cos + im * phase_sin)
            stack.append(im * phase_cos - re * phase_sin)
        part = dot3(up, halves(jnp.concatenate(stack, axis=0)), NN).T
        for h in range(2):
            for t in range(own_blocks):
                first = h * LANES // 2 + t * SUB_DEV
                own_out[t, h * RADIX // 2 + k] = part[first : first + SUB_DEV]
                first += own_blocks * SUB_DEV
                pair_out[t, h * RADIX // 2 + k] = part[first : first + SUB_DEV]
    store.wait()


def predict_kernel(counts_ref, x0, x1, x2, x3, a_ref, b_ref, out_ref, *, scale):
    total = (x0[...] + x1[...]) + (x2[...] + x3[...])
    slot = lax.broadcasted_iota(jnp.int32, (1, CAP), 1)
    for j in range(SUB_DEV):
        rows = total[:, j, :]
        left = halves(jnp.concatenate([rows[:, : LANES // 2], rows[:, LANES // 2 :]], axis=0))
        a_re, a_im = a_ref[j, :SG], a_ref[j, SG:]
        inner_re = dot3(left, halves(jnp.concatenate([a_re, a_im], axis=0)), NN)
        inner_im = dot3(left, halves(jnp.concatenate([-a_im, a_re], axis=0)), NN)
        b_re, b_im = b_ref[j, :SG], b_ref[j, SG:]
        factor = jnp.where(slot < counts_ref[j], scale, 0.0)
        re = jnp.sum(b_re * inner_re + b_im * inner_im, axis=0, keepdims=True)
        im = jnp.sum(b_re * inner_im - b_im * inner_re, axis=0, keepdims=True)
        out_ref[0, j : j + 1] = re * factor
        out_ref[1, j : j + 1] = im * factor


def swap(x, axis, mask):
    size = lax.axis_size(axis)
    return lax.ppermute(x, axis, [(i, i ^ mask) for i in range(size)])


def fast_device(
    visibilities, uv_offset, chan_index, counts, row_tile, col_tile, primary_beam, model_image
):
    shards = lax.axis_size("chan")
    owners = lax.axis_size("sub")
    rows, facet_len = primary_beam.shape
    f32 = jnp.float32
    vmem = pl.BlockSpec(memory_space=pltpu.VMEM)
    smem = pl.BlockSpec(memory_space=pltpu.SMEM)
    hbm = pl.BlockSpec(memory_space=pl.ANY)
    keep = lambda x: pltpu.with_memory_space_constraint(x, pltpu.VMEM)
    counts = counts.reshape(SUB_DEV)
    payload, a_rows, b_rows = pl.pallas_call(
        functools.partial(grid_kernel, shards=shards, row_tiles=facet_len // owners // SG),
        out_shape=(
            pltpu.VMEM((RADIX + 1, SUB_DEV, LANES), f32),
            pltpu.VMEM((SUB_DEV, 2 * SG, CAP), f32),
            pltpu.VMEM((SUB_DEV, 2 * SG, CAP), f32),
        ),
        in_specs=[smem] * 3 + [vmem] * 4,
        out_specs=[vmem] * 3,
        name="grid",
    )(row_tile, col_tile, counts, visibilities, uv_offset, chan_index, window_table())
    block = lax.axis_index("chan") * owners + lax.axis_index("sub")
    table = lax.dynamic_index_in_dim(jnp.asarray(column_table(facet_len, rows)), block, 0, False)
    payload = payload + sum(swap(payload, "chan", k) for k in range(1, shards))
    own = jnp.stack([payload] + [swap(payload, "sub", k) for k in range(2, owners, 2)])
    pair = swap(own, "sub", 1)
    part = pltpu.VMEM((owners // 2, RADIX, SUB_DEV, LANES), f32)
    new_model, own, pair = pl.pallas_call(
        functools.partial(
            image_kernel,
            shards=shards,
            scale=1.0 / (SG * SG * math.sqrt(SUB_DEV * owners * CAP * shards)),
        ),
        out_shape=(jax.ShapeDtypeStruct((rows, facet_len), f32), part, part),
        in_specs=[vmem] * 3 + [hbm] * 2,
        out_specs=[hbm, vmem, vmem],
        scratch_shapes=[
            pltpu.VMEM((2, RADIX * rows, 2 * LANES), jnp.bfloat16),
            pltpu.VMEM((RADIX * rows, 2 * LANES), f32),
            pltpu.VMEM((RADIX * rows, 2 * LANES), f32),
            pltpu.VMEM((rows, facet_len), f32),
            pltpu.VMEM((rows, facet_len), f32),
            pltpu.VMEM((rows, facet_len), f32),
            pltpu.SemaphoreType.DMA((3,)),
        ],
        name="image",
    )(keep(own), keep(pair), keep(table), primary_beam, model_image)
    own = own + swap(pair, "sub", 1)
    part = own[0] + sum(swap(own[k // 2], "sub", k) for k in range(2, owners, 2))
    parts = [part] + [swap(part, "chan", k) for k in range(1, shards)]
    predicted = pl.pallas_call(
        functools.partial(predict_kernel, scale=4.0 / SG / SG / facet_len),
        out_shape=jax.ShapeDtypeStruct((2, SUB_DEV, CAP), f32),
        in_specs=[smem] + [vmem] * 6,
        out_specs=vmem,
        name="predict",
    )(counts, *map(keep, parts), keep(a_rows), keep(b_rows))
    return new_model, predicted


def on_device(*arrays):
    shards, owners = lax.axis_size("chan"), lax.axis_size("sub")
    rows, facet_len = arrays[6].shape
    fits = (
        shards == 4
        and owners == 8
        and 2 * rows == LANES
        and facet_len == RADIX * LANES
        and 2 * owners * SUB_DEV == LANES
    )
    return (fast_device if fits else general_device)(*arrays)


def solution(mesh):
    in_specs = (
        P(None, "sub", "chan"),
        P(None, "sub", "chan"),
        P("sub", "chan"),
        P("sub", "chan"),
        P("sub"),
        P("sub"),
        P(("chan", "sub"), None),
        P(("chan", "sub"), None),
    )
    out_specs = (P(("chan", "sub"), None), P(None, "sub", "chan"))
    return jax.shard_map(
        on_device, mesh=mesh, in_specs=in_specs, out_specs=out_specs, check_vma=False
    )
```
